256 devices in a mesh: ctx: 8 (over x, z_hi), chan: 8 (over z_lo, core), rep: 4 (over y).
Axes of the slice: x: 4, y: 4, z: 8 (z_hi: 2, z_lo: 4; z = z_hi * 4 + z_lo), core: 2. Of those that a mesh axis runs over, the one named last changes fastest.
Arguments:
- values_in: bfloat16 [4, 2048, 4096], P('rep', 'ctx', 'chan'), may hold values from -6 to 6
- keys_in: bfloat16 [4, 2048, 4096], P('rep', 'ctx', 'chan'), may hold values from -6 to 6
- query_in: bfloat16 [4, 2048, 4096], P('rep', 'ctx', 'chan'), may hold values from -6 to 6
- cotangent: bfloat16 [4, 2048, 4096], P('rep', 'ctx', 'chan'), may hold values from -6 to 6
- out_weight: bfloat16 [4096, 4096], P(None, 'chan'), may hold values from -0.09375 to 0.09375
- residues: float32 [16, 256], P(None, 'chan'), may hold values from -0.2581989 to 0.2581989
- rates: float32 [16, 256], P(None, 'chan'), may hold values from 9.765625e-05 to 0.0333333333
Outputs:
- output: bfloat16 [4, 2048, 4096], P('rep', 'ctx', 'chan')
- grad_values: bfloat16 [4, 2048, 4096], P('rep', 'ctx', 'chan')
- grad_keys: bfloat16 [4, 2048, 4096], P('rep', 'ctx', 'chan')
- grad_query: bfloat16 [4, 2048, 4096], P('rep', 'ctx', 'chan')
- grad_residues: float32 [16, 256], P(None, 'chan')
- grad_rates: float32 [16, 256], P(None, 'chan')
The draws below stay inside these ranges and needn't reach their ends.
All inputs are finite; a program needn't handle non-finite values.
Results may differ from the reference program's by a relative error of at most 0.013.
Values may be sent and summed in bfloat16 or wider, within the bound.
A program may use at most 128 MiB of HBM per device.

```python
import jax
import jax.numpy as jnp
from jax import lax

GROUP = 16
POLES = 16
SEQ = 2048
CHANNELS = 4096
GROUPS = 256
BATCH = 4


def pole_table(key):
    base = jax.random.fold_in(key, 4711)
    key_pick, key_rate, key_amp = jax.random.split(base, 3)
    shape = (POLES, GROUPS)
    pick = jax.random.randint(key_pick, shape, 0, 10)
    slow_mask = pick < 5
    unit = jax.random.uniform(key_rate, shape, jnp.float32)
    slow_rate = jnp.exp(jnp.log(0.2 / SEQ) + unit * jnp.log(10.0))
    fast_rate = jnp.exp(jnp.log(1.0 / 50.0) + unit * jnp.log(50.0 / 30.0))
    rate_vals = jnp.where(slow_mask, slow_rate, fast_rate)
    amp = jnp.clip(jax.random.normal(key_amp, shape, jnp.float32), -4.0, 4.0)
    residue_vals = amp * jnp.sqrt(2.0 * rate_vals / POLES)
    return (residue_vals, rate_vals)


def draw_residues(key, part):
    return pole_table(key)[0]


def draw_rates(key, part):
    return pole_table(key)[1]


def block_levels(rng, dims, shards, low, largest):
    loudness = 1.0
    for axis_at, blocks in shards:
        steps = jax.random.uniform(jax.random.fold_in(jax.random.fold_in(rng, 6), axis_at), (blocks,), jnp.float32, low / len(shards), largest / len(shards))
        loudness = loudness * jnp.repeat(jnp.exp(steps), dims[axis_at] // blocks).reshape((-1,) + (1,) * (len(dims) - 1 - axis_at))
    return loudness


def gaussian(stream_key, dims, width, limit, shards=(), kind=jnp.bfloat16):
    result = width * jax.random.normal(stream_key, dims, jnp.float32)
    if shards:
        result = result * block_levels(stream_key, dims, shards, -0.22, 0.18)
    return jnp.clip(result, -limit, limit).astype(kind)


def setup_inputs(seed: int = 0) -> dict:
    streams_of = jax.random.split(jax.random.key(seed), 8)
    values_in = gaussian(streams_of[0], (BATCH, SEQ, CHANNELS), 1.0, 6.0, ((0, 4), (1, 8), (2, 8)))
    keys_in = gaussian(streams_of[1], (BATCH, SEQ, CHANNELS), 1.0, 6.0, ((0, 4), (1, 8), (2, 8)))
    query_in = gaussian(streams_of[2], (BATCH, SEQ, CHANNELS), 1.0, 6.0, ((0, 4), (1, 8), (2, 8)))
    cotangent = gaussian(streams_of[3], (BATCH, SEQ, CHANNELS), 1.0, 6.0, ((0, 4), (1, 8), (2, 8)))
    out_weight = gaussian(streams_of[4], (CHANNELS, CHANNELS), CHANNELS ** -0.5, 0.09375, ((1, 8),))
    residues = draw_residues(jax.random.fold_in(streams_of[7], 71), 0)
    rates = draw_rates(jax.random.fold_in(streams_of[7], 71), 0)
    return dict(values_in=values_in, keys_in=keys_in, query_in=query_in, cotangent=cotangent, out_weight=out_weight, residues=residues, rates=rates)


def causal_conv(signal, taps):
    length = signal.shape[0]
    total = 2 * length
    spectrum = jnp.fft.rfft(signal, total, axis=0) * jnp.fft.rfft(taps, total, axis=0)
    return jnp.fft.irfft(spectrum, total, axis=0)[:length]


def correlate(later, earlier):
    length = later.shape[0]
    total = 2 * length
    spectrum = jnp.fft.rfft(later, total, axis=0) * jnp.conj(jnp.fft.rfft(earlier, total, axis=0))
    return jnp.fft.irfft(spectrum, total, axis=0)[:length]


def reference(values_in, keys_in, query_in, cotangent, out_weight, residues, rates):
    highest = lax.Precision.HIGHEST
    lag_pos = jnp.arange(SEQ).astype(jnp.float32)
    decay_table = jnp.exp(-lag_pos[:, None, None] * rates[None])
    filter_taps = jnp.einsum('lrg,rg->lg', decay_table, residues, precision=highest)
    channel_taps = jnp.repeat(filter_taps, GROUP, axis=1)

    def one_sequence(items):
        v_seq, k_seq, q_seq, d_seq = items
        k_float = k_seq.astype(jnp.float32)
        v_float = v_seq.astype(jnp.float32)
        q_float = q_seq.astype(jnp.float32)
        z_round = lax.optimization_barrier((k_float * v_float).astype(jnp.bfloat16))
        z_float = z_round.astype(jnp.float32)
        conv = causal_conv(z_float, channel_taps)
        gated = (q_float * conv).astype(jnp.bfloat16)
        output = jnp.dot(gated, out_weight.T, preferred_element_type=jnp.float32).astype(jnp.bfloat16)
        back = jnp.dot(d_seq, out_weight, preferred_element_type=jnp.float32)
        dconv = q_float * back
        grad_q = (conv * back).astype(jnp.bfloat16)
        dz_field = causal_conv(dconv[::-1], channel_taps)[::-1]
        grad_v = (dz_field * k_float).astype(jnp.bfloat16)
        grad_k = (dz_field * v_float).astype(jnp.bfloat16)
        lag_corr = correlate(dconv, z_float)
        lag_group = lag_corr.reshape(SEQ, GROUPS, GROUP).sum(axis=2)
        return output, grad_v, grad_k, grad_q, lag_group

    output, grad_values, grad_keys, grad_query, lag_all = lax.map(one_sequence, (values_in, keys_in, query_in, cotangent))
    lag_sums = jnp.sum(lag_all, axis=0)
    grad_residues = jnp.einsum('lg,lrg->rg', lag_sums, decay_table, precision=highest)
    grad_rates = -residues * jnp.einsum('lg,lrg->rg', lag_sums * lag_pos[:, None], decay_table, precision=highest)
    return output, grad_values, grad_keys, grad_query, grad_residues, grad_rates
```

```python
import functools

import jax
import jax.numpy as jnp
from jax import lax
from jax.experimental import pallas as pl
from jax.experimental.pallas import tpu as pltpu
from jax.sharding import PartitionSpec as P

GROUP = 16
F32 = jnp.float32
BF16 = jnp.bfloat16
MESH = pl.DeviceIdType.MESH


def iota(shape, axis):
    return lax.broadcasted_iota(jnp.int32, shape, axis)


def dot(a, b, ca=1, cb=0):
    return lax.dot_general(a, b, (((ca,), (cb,)), ((), ())), preferred_element_type=F32)


def dot_exact(a, b, ca=1, cb=0):
    return lax.dot_general(
        a, b, (((ca,), (cb,)), ((), ())), precision=lax.Precision.HIGHEST, preferred_element_type=F32
    )


def split(a):
    high = a.astype(BF16)
    return high, (a - high.astype(F32)).astype(BF16)


def kernel(
    v_ref, k_ref, q_ref, d_ref, w_hbm, rates_ref, res_ref,
    out_ref, gv_ref, gk_ref, gq_ref, gres_ref, grate_ref,
    w_ref, w_sem, own_sem,
    rate_col, res_col, rate_row, res_row, rate_chan,
    tab_u, tab_v, e_s, e_p, e_q, e_q1, row_f, row_b, row_v, row_u,
    z_ref, conv_ref, gated_ref, dconv_ref, back_ref, dz_ref,
    state_s, state_p, pair_s, pair_p, zin_s, zin_p, xin_s, xin_p, in_s, in_p,
    state_q, state_q1, pair_q, zin_q, xin_q, in_q,
    g_own, g_par, pacc, pbuf, xbuf, snd_r, snd_l, rec_l, rec_r,
    gsum, gout, gin_y, gin_x, gin_z,
    ag_send, ag_recv, agp_send, agp_recv,
    fz_send, fz_recv, fx_send, fx_recv, bx_send, bx_recv,
    p_send, p_recv, rr_send, rr_recv, rl_send, rl_recv, gs_send, gs_recv,
):
    chan = lax.axis_index("chan")
    ctx = lax.axis_index("ctx")
    rep = lax.axis_index("rep")
    core, zl = lax.rem(chan, 2), lax.div(chan, 2)
    zh, xx = lax.rem(ctx, 2), lax.div(ctx, 2)
    has_left, has_right = zl > 0, zl < 3
    left, right, partner = {"chan": chan - 2}, {"chan": chan + 2}, {"chan": chan + 1 - 2 * core}
    zpeer = {"ctx": ctx + 1 - 2 * zh}
    xpeer = [{"ctx": lax.rem(xx + i, 4) * 2 + zh} for i in (1, 2, 3)]
    ypeer = [{"rep": lax.rem(rep + i, 4)} for i in (1, 2, 3)]

    def remote(src, dst, ssem, rsem, dev):
        return pltpu.make_async_remote_copy(
            src_ref=src, dst_ref=dst, send_sem=ssem, recv_sem=rsem, device_id=dev, device_id_type=MESH
        )

    w_copy = pltpu.make_async_copy(w_hbm, w_ref, w_sem)
    w_copy.start()
    own_copy = pltpu.make_async_copy(d_ref, g_own.at[zl], own_sem)
    own_copy.start()
    barrier = pltpu.get_barrier_semaphore()
    for dev in [partner, zpeer] + xpeer + ypeer:
        pl.semaphore_signal(barrier, inc=1, device_id=dev, device_id_type=MESH)

    @pl.when(has_left)
    def _():
        pl.semaphore_signal(barrier, inc=1, device_id=left, device_id_type=MESH)

    @pl.when(has_right)
    def _():
        pl.semaphore_signal(barrier, inc=1, device_id=right, device_id_type=MESH)

    sel_col = jnp.where(lax.div(iota((512, 32), 0), 16) == iota((512, 32), 1), 1.0, 0.0).astype(F32)
    own_col = lax.rem(iota((512, 16), 0), 16) == iota((512, 16), 1)
    sel_row = jnp.where(lax.div(iota((32, 512), 1), 16) == iota((32, 512), 0), 1.0, 0.0).astype(F32)
    own_row = lax.rem(iota((16, 512), 1), 16) == iota((16, 512), 0)
    for src, col, row in ((rates_ref, rate_col, rate_row), (res_ref, res_col, res_row)):
        wide = dot_exact(sel_col, src[...], 1, 1)
        col[...] = jnp.sum(jnp.where(own_col, wide, 0.0), axis=1, keepdims=True)
        flat = dot_exact(src[...], sel_row)
        row[...] = jnp.sum(jnp.where(own_row, flat, 0.0), axis=0, keepdims=True)
        if src is rates_ref:
            rate_chan[...] = flat

    lane256 = iota((64, 256), 1).astype(F32)

    @pl.loop(0, 8)
    def _(i):
        rows = pl.ds(pl.multiple_of(i * 64, 64), 64)
        rate = rate_col[rows, :]
        left_over = 256.0 - lane256
        decay = jnp.exp(-rate * left_over)
        high, low = split(decay)
        e_s[0, rows, :] = high
        e_s[1, rows, :] = low
        e_p[rows, :] = (decay * left_over).astype(BF16)

    z_ref[...] = (k_ref[...].astype(F32) * v_ref[...].astype(F32)).astype(BF16)
    own_block = lax.div(iota((256, 256), 0), 16) == lax.div(iota((256, 256), 1), 16)

    def fold(a):
        return jnp.sum(jnp.where(own_block, a, 0.0).reshape(16, 16, 256), axis=0)

    def spread(s):
        return jnp.where(own_block, jnp.broadcast_to(s[None], (16, 16, 256)).reshape(256, 256), 0.0)

    for tile in range(2):
        part = slice(tile * 256, tile * 256 + 256)
        zt = z_ref[:, part]
        state_s[:, part] = fold(dot(e_s[0, part, :], zt) + dot(e_s[1, part, :], zt))
        state_p[:, part] = fold(dot(e_p[part, :], zt))

    pl.semaphore_wait(barrier, 8 + jnp.where(has_left, 1, 0) + jnp.where(has_right, 1, 0))

    fz = [
        remote(state_s, zin_s, fz_send.at[0], fz_recv.at[0], zpeer),
        remote(state_p, zin_p, fz_send.at[1], fz_recv.at[1], zpeer),
    ]
    for c in fz:
        c.start()

    def ag_right(src_ref, src, m):
        return remote(src_ref, g_own.at[src], ag_send.at[0, m], ag_recv.at[src], right)

    def ag_left(src_ref, src, m):
        return remote(src_ref, g_own.at[src], ag_send.at[1, m], ag_recv.at[src], left)

    def ag_partner(src_ref, src):
        return remote(src_ref, g_par.at[src], agp_send.at[src], agp_recv.at[src], partner)

    @pl.when(has_right)
    def _():
        ag_right(d_ref, zl, 0).start()

    @pl.when(has_left)
    def _():
        ag_left(d_ref, zl, 0).start()

    ag_partner(d_ref, zl).start()

    def ag_step(m):
        src_l, src_r = zl - m, zl + m

        @pl.when(src_l >= 0)
        def _():
            ag_right(g_own.at[src_l], src_l, 0).wait_recv()

            if m < 3:
                @pl.when(has_right)
                def _():
                    ag_right(g_own.at[src_l], src_l, m).start()

            ag_partner(g_own.at[src_l], src_l).start()

        @pl.when(src_r <= 3)
        def _():
            ag_left(g_own.at[src_r], src_r, 0).wait_recv()

            if m < 3:
                @pl.when(has_left)
                def _():
                    ag_left(g_own.at[src_r], src_r, m).start()

            ag_partner(g_own.at[src_r], src_r).start()

    def ag_drain():
        for m in range(3):
            @pl.when(jnp.logical_and(has_right, zl - m >= 0))
            def _():
                ag_right(d_ref, zl, m).wait_send()

            @pl.when(jnp.logical_and(has_left, zl + m <= 3))
            def _():
                ag_left(d_ref, zl, m).wait_send()

        for j in range(4):
            ag_partner(d_ref, j).wait_send()

    @pl.loop(0, 8)
    def _(i):
        rows = pl.ds(pl.multiple_of(i * 64, 64), 64)
        groups = pl.ds(i * 4, 4)
        rate, res = rate_col[rows, :], res_col[rows, :]
        centre = lane256 - 128.0
        u_high, u_low = split(res * jnp.exp(-rate * centre))
        v_high, v_low = split(jnp.exp(rate * centre))
        for at, uu, vv in ((0, u_high, v_high), (16, u_high, v_low), (32, u_low, v_high)):
            tab_u[groups, at : at + 16, :] = uu.reshape(4, 16, 256)
            tab_v[groups, at : at + 16, :] = vv.reshape(4, 16, 256)

    token = iota((256, 256), 0)
    other = iota((256, 256), 1)
    lane_group = lax.div(other, 16)

    def conv_tile(tile):
        part = slice(tile * 256, tile * 256 + 256)
        conv_ref[:, part] = jnp.zeros((256, 256), F32)

        @pl.loop(0, 16)
        def _(g):
            at = tile * 16 + g
            taps = jnp.where(token >= other, dot(tab_u[at], tab_v[at], 0, 0), 0.0).astype(BF16)
            masked = jnp.where(lane_group == g, z_ref[:, part].astype(F32), 0.0).astype(BF16)
            conv_ref[:, part] += dot(taps, masked)

    conv_tile(0)

    slab_decay = jnp.exp(-256.0 * rate_chan[...])
    for c in fz:
        c.wait_recv()
    first = zh == 0
    s_one = jnp.where(first, state_s[...], zin_s[...])
    s_two = jnp.where(first, zin_s[...], state_s[...])
    p_one = jnp.where(first, state_p[...], zin_p[...])
    p_two = jnp.where(first, zin_p[...], state_p[...])
    pair_s[...] = slab_decay * s_one + s_two
    pair_p[...] = slab_decay * (p_one + 256.0 * s_one) + p_two
    fx = []
    for i in range(3):
        fx.append(remote(pair_s, xin_s.at[i], fx_send.at[0, i], fx_recv.at[0, i], xpeer[i]))
        fx[-1].start()
    for i in range(3):
        fx.append(remote(pair_p, xin_p.at[i], fx_send.at[1, i], fx_recv.at[1, i], xpeer[i]))
        fx[-1].start()

    conv_tile(1)
    ag_step(1)

    @pl.loop(0, 4)
    def _(i):
        rows = pl.ds(pl.multiple_of(i * 64, 64), 64)
        at = (iota((64, 512), 0) + i * 64).astype(F32)
        rate, res = rate_row[...], res_row[...]
        f_high, f_low = split(res * jnp.exp(-rate * at))
        row_f[0, rows, :] = f_high
        row_f[1, rows, :] = f_low
        b_high, b_low = split(res * jnp.exp(-rate * (256.0 - at)))
        row_b[0, rows, :] = b_high
        row_b[1, rows, :] = b_low
        centre = at - 128.0
        up = jnp.exp(rate * centre)
        row_v[0, rows, :] = up.astype(BF16)
        row_v[1, rows, :] = (up * centre).astype(BF16)
        row_u[rows, :] = jnp.exp(-rate * centre)

    @pl.loop(0, 8)
    def _(i):
        rows = pl.ds(pl.multiple_of(i * 64, 64), 64)
        decay = jnp.exp(-rate_col[rows, :] * lane256)
        high, low = split(decay)
        e_q[0, rows, :] = high
        e_q[1, rows, :] = low
        e_q1[rows, :] = (decay * lane256).astype(BF16)

    for c in fx:
        c.wait_recv()
    sum_s = jnp.where(first, 0.0, zin_s[...])
    sum_p = jnp.where(first, 0.0, zin_p[...])
    for i in range(3):
        gap = 256.0 * (2 * i + zh).astype(F32)
        earlier = xx >= i + 1
        weight = jnp.exp(-gap * rate_chan[...])
        sum_s += jnp.where(earlier, weight * xin_s[i], 0.0)
        sum_p += jnp.where(earlier, weight * (xin_p[i] + gap * xin_s[i]), 0.0)
    in_s[...] = sum_s
    in_p[...] = sum_p

    def carried(rows, state, part):
        s_high, s_low = split(spread(state[:, part]))
        return (
            dot(rows[0, :, part], s_high) + dot(rows[1, :, part], s_high) + dot(rows[0, :, part], s_low)
        )

    for tile in range(2):
        part = slice(tile * 256, tile * 256 + 256)
        conv = conv_ref[:, part] + carried(row_f, in_s, part)
        conv_ref[:, part] = conv
        gated_ref[:, part] = (q_ref[:, part].astype(F32) * conv).astype(BF16)

    w_copy.wait()
    own_copy.wait()

    def w_block(j, a):
        return w_ref[pl.ds(pl.multiple_of((2 * j + a) * 512, 512), 512), :]

    def to_partner(j):
        return remote(pbuf.at[j], xbuf.at[j], p_send.at[j], p_recv.at[j], partner)

    @pl.loop(0, 4)
    def _(j):
        pbuf[j] = dot(gated_ref[...], w_block(j, 1 - core), 1, 1).astype(BF16)
        to_partner(j).start()

    @pl.loop(0, 4)
    def _(j):
        pacc[j] = dot(gated_ref[...], w_block(j, core), 1, 1)

    ag_step(2)

    @pl.loop(0, 4)
    def _(j):
        to_partner(j).wait_recv()
        pacc[j] += xbuf[j].astype(F32)

    def rs_right(j):
        return remote(snd_r.at[j], rec_l.at[j], rr_send.at[j], rr_recv.at[j], right)

    def rs_left(j):
        return remote(snd_l.at[j], rec_r.at[j], rl_send.at[j], rl_recv.at[j], left)

    def rs_step(m, end):
        jr, jl = 3 - m, m
        if end == 0:
            @pl.when(jnp.logical_and(jr > zl, zl == 0))
            def _():
                snd_r[jr] = pacc[jr].astype(BF16)
                rs_right(jr).start()

            @pl.when(jnp.logical_and(jl < zl, zl == 3))
            def _():
                snd_l[jl] = pacc[jl].astype(BF16)
                rs_left(jl).start()
        else:
            @pl.when(jnp.logical_and(jr > zl, zl > 0))
            def _():
                rs_right(jr).wait_recv()
                snd_r[jr] = (pacc[jr] + rec_l[jr].astype(F32)).astype(BF16)
                rs_right(jr).start()

            @pl.when(jnp.logical_and(jl < zl, zl < 3))
            def _():
                rs_left(jl).wait_recv()
                snd_l[jl] = (pacc[jl] + rec_r[jl].astype(F32)).astype(BF16)
                rs_left(jl).start()

    for m in range(3):
        rs_step(m, 0)

    ag_step(3)

    back_ref[...] = jnp.zeros((256, 512), F32)

    @pl.loop(0, 4)
    def _(j):
        back_ref[...] += dot(g_own[j], w_block(j, core))

    for j in range(4):
        ag_partner(d_ref, j).wait_recv()

    @pl.loop(0, 4)
    def _(j):
        back_ref[...] += dot(g_par[j], w_block(j, 1 - core))

    dconv_ref[...] = (q_ref[...].astype(F32) * back_ref[...]).astype(BF16)
    gq_ref[...] = (conv_ref[...] * back_ref[...]).astype(BF16)
    for tile in range(2):
        part = slice(tile * 256, tile * 256 + 256)
        dt = dconv_ref[:, part]
        state_q[:, part] = fold(dot(e_q[0, part, :], dt) + dot(e_q[1, part, :], dt))
        state_q1[:, part] = fold(dot(e_q1[part, :], dt))
    bz = remote(state_q, zin_q, fz_send.at[2], fz_recv.at[2], zpeer)
    bz.start()

    rs_step(0, 1)
    gsum[...] = jnp.zeros((8, 512), F32)

    def back_tile(tile):
        part = slice(tile * 256, tile * 256 + 256)
        dz_ref[:, part] = jnp.zeros((256, 256), F32)

        @pl.loop(0, 16)
        def _(g):
            at = tile * 16 + g
            taps = jnp.where(other >= token, dot(tab_v[at], tab_u[at], 0, 0), 0.0).astype(BF16)
            masked = jnp.where(lane_group == g, dconv_ref[:, part].astype(F32), 0.0).astype(BF16)
            dz_ref[:, part] += dot(taps, masked)
            mixed = jnp.where(token >= other, dot(masked, z_ref[:, part], 1, 1), 0.0).astype(BF16)
            first_sum = dot(mixed, row_v[0, :, part]) * row_u[:, part]
            second_sum = dot(mixed, row_v[1, :, part]) * row_u[:, part]
            centre = (token - 128).astype(F32)
            by_res = jnp.sum(first_sum.reshape(32, 8, 256), axis=0)
            by_rate = jnp.sum((first_sum * centre - second_sum).reshape(32, 8, 256), axis=0)
            mine = lax.div(iota((8, 256), 1), 16) == g
            gsum[:, part] += jnp.where(mine, by_res, 0.0)
            gout[:, part] += jnp.where(mine, by_rate, 0.0)

    gout[...] = jnp.zeros((8, 512), F32)
    back_tile(0)
    rs_step(1, 1)

    bz.wait_recv()
    q_one = jnp.where(first, state_q[...], zin_q[...])
    q_two = jnp.where(first, zin_q[...], state_q[...])
    pair_q[...] = q_one + slab_decay * q_two
    bx = []
    for i in range(3):
        bx.append(remote(pair_q, xin_q.at[i], bx_send.at[i], bx_recv.at[i], xpeer[i]))
        bx[-1].start()

    back_tile(1)
    rs_step(2, 1)

    fold_chan = sel_row
    by_res = dot_exact(state_q[...] * in_s[...], fold_chan, 1, 1)
    by_rate = dot_exact(state_q1[...] * in_s[...] + state_q[...] * in_p[...], fold_chan, 1, 1)
    flat_res = jnp.sum(gsum[...], axis=0, keepdims=True)
    flat_rate = jnp.sum(gout[...], axis=0, keepdims=True)
    by_res += dot_exact(jnp.where(own_row, flat_res, 0.0), fold_chan, 1, 1)
    by_rate += dot_exact(jnp.where(own_row, flat_rate, 0.0), fold_chan, 1, 1)
    gin_z[0] = jnp.zeros((32, 128), F32)
    gin_z[0, 0:16, 0:32] = by_res
    gin_z[0, 16:32, 0:32] = by_rate

    def exchange(src, dst, at, peers):
        copies = []
        for i, dev in enumerate(peers):
            copies.append(remote(src, dst.at[i], gs_send.at[at + i], gs_recv.at[at + i], dev))
            copies[-1].start()
        return copies

    started = exchange(gin_z.at[0], gin_y, 0, ypeer)

    for c in bx:
        c.wait_recv()
    sum_q = jnp.where(first, zin_q[...], 0.0)
    for i in range(3):
        steps = 4 - (i + 1)
        later = xx + steps <= 3
        gap = 256.0 * (2 * (steps - 1) + 1 - zh).astype(F32)
        sum_q += jnp.where(later, jnp.exp(-gap * rate_chan[...]) * xin_q[i], 0.0)
    in_q[...] = sum_q
    for tile in range(2):
        part = slice(tile * 256, tile * 256 + 256)
        dz = dz_ref[:, part] + carried(row_b, in_q, part)
        gv_ref[:, part] = (dz * k_ref[:, part].astype(F32)).astype(BF16)
        gk_ref[:, part] = (dz * v_ref[:, part].astype(F32)).astype(BF16)

    for c in started:
        c.wait_recv()
    gin_z[1] = gin_z[0] + gin_y[0] + gin_y[1] + gin_y[2]
    more = exchange(gin_z.at[1], gin_x, 3, xpeer)
    for c in more:
        c.wait_recv()
    started += more
    gin_z[2] = gin_z[1] + gin_x[0] + gin_x[1] + gin_x[2]
    last = remote(gin_z.at[2], gin_z.at[3], gs_send.at[6], gs_recv.at[6], zpeer)
    last.start()

    @pl.when(has_left)
    def _():
        rs_right(zl).wait_recv()
        pacc[zl] += rec_l[zl].astype(F32)

    @pl.when(has_right)
    def _():
        rs_left(zl).wait_recv()
        pacc[zl] += rec_r[zl].astype(F32)

    out_ref[...] = pacc[zl].astype(BF16)

    last.wait_recv()
    total = gin_z[2] + gin_z[3]
    gres_ref[...] = total[0:16, 0:32]
    grate_ref[...] = -res_ref[...] * total[16:32, 0:32]

    for c in fz + fx + bx + [bz, last] + started:
        c.wait_send()
    ag_drain()
    for j in range(4):
        to_partner(j).wait_send()

        @pl.when(j > zl)
        def _():
            rs_right(j).wait_send()

        @pl.when(j < zl)
        def _():
            rs_left(j).wait_send()


def per_device(values_in, keys_in, query_in, cotangent, out_weight, residues, rates):
    vm = pltpu.VMEM
    dma = pltpu.SemaphoreType.DMA
    act = jax.ShapeDtypeStruct((256, 512), BF16)
    par = jax.ShapeDtypeStruct((16, 32), F32)
    spec = pl.BlockSpec(memory_space=pltpu.VMEM)
    blocks = lambda: vm((4, 256, 512), BF16)
    state = lambda: vm((16, 512), F32)
    states = lambda: vm((3, 16, 512), F32)
    scratch = [
        vm((4096, 512), BF16), dma, dma,
        vm((512, 1), F32), vm((512, 1), F32), vm((1, 512), F32), vm((1, 512), F32), state(),
        vm((32, 48, 256), BF16), vm((32, 48, 256), BF16),
        vm((2, 512, 256), BF16), vm((512, 256), BF16), vm((2, 512, 256), BF16), vm((512, 256), BF16),
        vm((2, 256, 512), BF16), vm((2, 256, 512), BF16), vm((2, 256, 512), BF16), vm((256, 512), F32),
        vm((256, 512), BF16), vm((256, 512), F32), vm((256, 512), BF16), vm((256, 512), BF16),
        vm((256, 512), F32), vm((256, 512), F32),
        state(), state(), state(), state(), state(), state(), states(), states(), state(), state(),
        state(), state(), state(), state(), states(), state(),
        blocks(), blocks(), vm((4, 256, 512), F32), blocks(), blocks(), blocks(), blocks(), blocks(), blocks(),
        vm((8, 512), F32), vm((8, 512), F32),
        vm((3, 32, 128), F32), vm((3, 32, 128), F32), vm((4, 32, 128), F32),
        dma((2, 3)), dma((4,)), dma((4,)), dma((4,)),
        dma((3,)), dma((3,)), dma((2, 3)), dma((2, 3)), dma((3,)), dma((3,)),
        dma((4,)), dma((4,)), dma((4,)), dma((4,)), dma((4,)), dma((4,)), dma((7,)), dma((7,)),
    ]
    out, gv, gk, gq, gres, grate = pl.pallas_call(
        kernel,
        out_shape=(act, act, act, act, par, par),
        in_specs=[spec, spec, spec, spec, pl.BlockSpec(memory_space=pl.ANY), spec, spec],
        out_specs=(spec,) * 6,
        scratch_shapes=scratch,
        compiler_params=pltpu.CompilerParams(
            collective_id=0, has_side_effects=True, vmem_limit_bytes=60 * 1024 * 1024
        ),
        name="hyena",
    )(values_in[0], keys_in[0], query_in[0], cotangent[0], out_weight, rates, residues)
    return out[None], gv[None], gk[None], gq[None], gres, grate


def solution(mesh):
    act = P("rep", "ctx", "chan")
    par = P(None, "chan")
    return jax.shard_map(
        per_device,
        mesh=mesh,
        in_specs=(act, act, act, act, par, par, par),
        out_specs=(act, act, act, act, par, par),
        check_vma=False,
    )
```

```python
import functools

import jax
import jax.numpy as jnp
from jax import lax
from jax.experimental import pallas as pl
from jax.experimental.pallas import tpu as pltpu
from jax.sharding import PartitionSpec as P

GROUP = 16
F32 = jnp.float32
BF16 = jnp.bfloat16
MESH = pl.DeviceIdType.MESH


def iota(shape, axis):
    return lax.broadcasted_iota(jnp.int32, shape, axis)


def dot(a, b, ca=1, cb=0):
    return lax.dot_general(a, b, (((ca,), (cb,)), ((), ())), preferred_element_type=F32)


def dot_exact(a, b, ca=1, cb=0):
    return lax.dot_general(
        a, b, (((ca,), (cb,)), ((), ())), precision=lax.Precision.HIGHEST, preferred_element_type=F32
    )


def split(a):
    high = a.astype(BF16)
    return high, (a - high.astype(F32)).astype(BF16)


def kernel(
    v_ref, k_ref, q_ref, d_ref, w_hbm, rates_ref, res_ref,
    out_ref, gv_ref, gk_ref, gq_ref, gres_ref, grate_ref,
    w_ref, w_sem, own_sem,
    rate_col, res_col, rate_row, res_row, rate_chan,
    tab_u, tab_v, tab_m, col_u, taps_back, z_mask, prod_res, prod_rate,
    e_s, e_p, e_q, e_q1, row_f, row_b,
    z_ref, conv_ref, gated_ref, dconv_ref, back_ref, dz_ref,
    state_s, state_p, pair_s, pair_p, zin_s, zin_p, xin_s, xin_p, in_s, in_p,
    state_q, state_q1, pair_q, zin_q, xin_q, in_q,
    g_own, g_par, pacc, pbuf, xbuf, snd_r, snd_l, rec_l, rec_r,
    gsum, gin_y, gin_c,
    ag_send, ag_recv, agp_send, agp_recv,
    fz_send, fz_recv, fx_send, fx_recv, bx_send, bx_recv,
    p_send, p_recv, rr_send, rr_recv, rl_send, rl_recv, gs_send, gs_recv,
):
    chan = lax.axis_index("chan")
    ctx = lax.axis_index("ctx")
    rep = lax.axis_index("rep")
    core, zl = lax.rem(chan, 2), lax.div(chan, 2)
    zh, xx = lax.rem(ctx, 2), lax.div(ctx, 2)
    has_left, has_right = zl > 0, zl < 3
    left, right, partner = {"chan": chan - 2}, {"chan": chan + 2}, {"chan": chan + 1 - 2 * core}
    zpeer = {"ctx": ctx + 1 - 2 * zh}
    xpeer = [{"ctx": lax.rem(xx + i, 4) * 2 + zh} for i in (1, 2, 3)]
    cpeer = [{"ctx": lax.rem(ctx + i, 8)} for i in range(1, 8)]
    ypeer = [{"rep": lax.rem(rep + i, 4)} for i in (1, 2, 3)]

    def remote(src, dst, ssem, rsem, dev):
        return pltpu.make_async_remote_copy(
            src_ref=src, dst_ref=dst, send_sem=ssem, recv_sem=rsem, device_id=dev, device_id_type=MESH
        )

    w_copy = pltpu.make_async_copy(w_hbm, w_ref, w_sem)
    w_copy.start()
    own_copy = pltpu.make_async_copy(d_ref, g_own.at[zl], own_sem)
    own_copy.start()
    barrier = pltpu.get_barrier_semaphore()
    for dev in [partner] + cpeer + ypeer:
        pl.semaphore_signal(barrier, inc=1, device_id=dev, device_id_type=MESH)

    @pl.when(has_left)
    def _():
        pl.semaphore_signal(barrier, inc=1, device_id=left, device_id_type=MESH)

    @pl.when(has_right)
    def _():
        pl.semaphore_signal(barrier, inc=1, device_id=right, device_id_type=MESH)

    sel_row = jnp.where(lax.div(iota((32, 512), 1), 16) == iota((32, 512), 0), 1.0, 0.0).astype(F32)
    own_row = lax.rem(iota((16, 512), 1), 16) == iota((16, 512), 0)
    for src, col, row in ((rates_ref, rate_col, rate_row), (res_ref, res_col, res_row)):
        flat = dot_exact(src[...], sel_row)
        line = jnp.sum(jnp.where(own_row, flat, 0.0), axis=0, keepdims=True)
        row[...] = line
        col[...] = jnp.transpose(jnp.broadcast_to(line, (128, 512)))
        if src is rates_ref:
            rate_chan[...] = flat

    def wide(ref, rows):
        return jnp.concatenate([ref[rows, :], ref[rows, :]], axis=1)

    lane256 = iota((64, 256), 1).astype(F32)

    @pl.loop(0, 8)
    def _(i):
        rows = pl.ds(pl.multiple_of(i * 64, 64), 64)
        rate = wide(rate_col, rows)
        left_over = 256.0 - lane256
        decay = jnp.exp(-rate * left_over)
        high, low = split(decay)
        e_s[0, rows, :] = high
        e_s[1, rows, :] = low
        e_p[rows, :] = (decay * left_over).astype(BF16)

    pl.semaphore_wait(barrier, 11 + jnp.where(has_left, 1, 0) + jnp.where(has_right, 1, 0))

    def half(h):
        return pl.ds(h * 128, 128)

    def ag_right(src_ref, src, m, h):
        return remote(
            src_ref.at[half(h)], g_own.at[src, half(h)], ag_send.at[0, m, h], ag_recv.at[src, h], right
        )

    def ag_left(src_ref, src, m, h):
        return remote(
            src_ref.at[half(h)], g_own.at[src, half(h)], ag_send.at[1, m, h], ag_recv.at[src, h], left
        )

    def ag_partner(src_ref, src, h):
        return remote(
            src_ref.at[half(h)], g_par.at[src, half(h)], agp_send.at[src, h], agp_recv.at[src, h], partner
        )

    for h in range(2):
        @pl.when(has_right)
        def _():
            ag_right(d_ref, zl, 0, h).start()

        @pl.when(has_left)
        def _():
            ag_left(d_ref, zl, 0, h).start()

    for h in range(2):
        ag_partner(d_ref, zl, h).start()

    def ag_step(m, h):
        src_l, src_r = zl - m, zl + m

        @pl.when(src_l >= 0)
        def _():
            ag_right(g_own.at[src_l], src_l, 0, h).wait_recv()

            if m < 3:
                @pl.when(has_right)
                def _():
                    ag_right(g_own.at[src_l], src_l, m, h).start()

            ag_partner(g_own.at[src_l], src_l, h).start()

        @pl.when(src_r <= 3)
        def _():
            ag_left(g_own.at[src_r], src_r, 0, h).wait_recv()

            if m < 3:
                @pl.when(has_left)
                def _():
                    ag_left(g_own.at[src_r], src_r, m, h).start()

            ag_partner(g_own.at[src_r], src_r, h).start()

    def ag_drain():
        for h in range(2):
            for m in range(3):
                @pl.when(jnp.logical_and(has_right, zl - m >= 0))
                def _():
                    ag_right(d_ref, zl, m, h).wait_send()

                @pl.when(jnp.logical_and(has_left, zl + m <= 3))
                def _():
                    ag_left(d_ref, zl, m, h).wait_send()

            for j in range(4):
                ag_partner(d_ref, j, h).wait_send()

    z_ref[...] = (k_ref[...].astype(F32) * v_ref[...].astype(F32)).astype(BF16)
    own_block = lax.div(iota((256, 256), 0), 16) == lax.div(iota((256, 256), 1), 16)

    def fold(a):
        return jnp.sum(jnp.where(own_block, a, 0.0).reshape(16, 16, 256), axis=0)

    def spread(s):
        return jnp.where(own_block, jnp.broadcast_to(s[None], (16, 16, 256)).reshape(256, 256), 0.0)

    for tile in range(2):
        part = slice(tile * 256, tile * 256 + 256)
        zt = z_ref[:, part]
        state_s[:, part] = fold(dot(e_s[0, part, :], zt) + dot(e_s[1, part, :], zt))
        state_p[:, part] = fold(dot(e_p[part, :], zt))

    fz = [
        remote(state_s, zin_s, fz_send.at[0], fz_recv.at[0], zpeer),
        remote(state_p, zin_p, fz_send.at[1], fz_recv.at[1], zpeer),
    ]
    for c in fz:
        c.start()

    @pl.loop(0, 8)
    def _(i):
        rows = pl.ds(pl.multiple_of(i * 64, 64), 64)
        groups = pl.ds(i * 4, 4)
        rate, res = wide(rate_col, rows), wide(res_col, rows)
        centre = lane256 - 128.0
        fall, rise = jnp.exp(-rate * centre), jnp.exp(rate * centre)
        u_high, u_low = split(res * fall)
        v_high, v_low = split(rise)
        for at, uu, vv in ((0, u_high, v_high), (16, u_high, v_low), (32, u_low, v_high)):
            tab_u[groups, at : at + 16, :] = uu.reshape(4, 16, 256)
            tab_v[groups, at : at + 16, :] = vv.reshape(4, 16, 256)
        tab_m[groups, 0:16, :] = v_high.reshape(4, 16, 256)
        tab_m[groups, 16:32, :] = (rise * centre).astype(BF16).reshape(4, 16, 256)
        col_u[rows, :] = fall

    token = iota((256, 256), 0)
    other = iota((256, 256), 1)
    lane_group = lax.div(other, 16)

    def conv_tile(tile, low, high):
        part = slice(tile * 256, tile * 256 + 256)

        @pl.loop(low, high)
        def _(i):
            for g in (2 * i, 2 * i + 1):
                at = tile * 16 + g
                taps = jnp.where(token >= other, dot(tab_u[at], tab_v[at], 0, 0), 0.0).astype(BF16)
                conv_ref[:, part] = jnp.where(
                    lane_group == g, dot(taps, z_ref[:, part]), conv_ref[:, part]
                )

    def taps_tile(tile):
        part = slice(tile * 256, tile * 256 + 256)

        @pl.loop(0, 8)
        def _(i):
            for g in (2 * i, 2 * i + 1):
                at = tile * 16 + g
                taps = jnp.where(other >= token, dot(tab_v[at], tab_u[at], 0, 0), 0.0)
                taps_back[at] = taps.astype(BF16)
                z_mask[at] = jnp.where(lane_group == g, z_ref[:, part].astype(F32), 0.0).astype(BF16)

    conv_tile(0, 0, 8)

    slab_decay = jnp.exp(-256.0 * rate_chan[...])
    for c in fz:
        c.wait_recv()
    first = zh == 0
    s_one = jnp.where(first, state_s[...], zin_s[...])
    s_two = jnp.where(first, zin_s[...], state_s[...])
    p_one = jnp.where(first, state_p[...], zin_p[...])
    p_two = jnp.where(first, zin_p[...], state_p[...])
    pair_s[...] = slab_decay * s_one + s_two
    pair_p[...] = slab_decay * (p_one + 256.0 * s_one) + p_two
    fx = []
    for i in range(3):
        fx.append(remote(pair_s, xin_s.at[i], fx_send.at[0, i], fx_recv.at[0, i], xpeer[i]))
        fx[-1].start()
    for i in range(3):
        fx.append(remote(pair_p, xin_p.at[i], fx_send.at[1, i], fx_recv.at[1, i], xpeer[i]))
        fx[-1].start()

    ag_step(1, 0)
    conv_tile(1, 0, 4)
    ag_step(1, 1)
    conv_tile(1, 4, 8)

    @pl.loop(0, 4)
    def _(i):
        rows = pl.ds(pl.multiple_of(i * 64, 64), 64)
        at = (iota((64, 512), 0) + i * 64).astype(F32)
        rate, res = rate_row[...], res_row[...]
        f_high, f_low = split(res * jnp.exp(-rate * at))
        row_f[0, rows, :] = f_high
        row_f[1, rows, :] = f_low
        b_high, b_low = split(res * jnp.exp(-rate * (256.0 - at)))
        row_b[0, rows, :] = b_high
        row_b[1, rows, :] = b_low

    @pl.loop(0, 8)
    def _(i):
        rows = pl.ds(pl.multiple_of(i * 64, 64), 64)
        decay = jnp.exp(-wide(rate_col, rows) * lane256)
        high, low = split(decay)
        e_q[0, rows, :] = high
        e_q[1, rows, :] = low
        e_q1[rows, :] = (decay * lane256).astype(BF16)

    ag_step(2, 0)
    for c in fx:
        c.wait_recv()
    sum_s = jnp.where(first, 0.0, zin_s[...])
    sum_p = jnp.where(first, 0.0, zin_p[...])
    for i in range(3):
        gap = 256.0 * (2 * i + zh).astype(F32)
        earlier = xx >= i + 1
        weight = jnp.exp(-gap * rate_chan[...])
        sum_s += jnp.where(earlier, weight * xin_s[i], 0.0)
        sum_p += jnp.where(earlier, weight * (xin_p[i] + gap * xin_s[i]), 0.0)
    in_s[...] = sum_s
    in_p[...] = sum_p

    def carried(rows, state, part):
        s_high, s_low = split(spread(state[:, part]))
        return (
            dot(rows[0, :, part], s_high) + dot(rows[1, :, part], s_high) + dot(rows[0, :, part], s_low)
        )

    for tile in range(2):
        part = slice(tile * 256, tile * 256 + 256)
        conv = conv_ref[:, part] + carried(row_f, in_s, part)
        conv_ref[:, part] = conv
        gated_ref[:, part] = (q_ref[:, part].astype(F32) * conv).astype(BF16)

    w_copy.wait()
    own_copy.wait()

    def w_block(j, a):
        return w_ref[pl.ds(pl.multiple_of((2 * j + a) * 512, 512), 512), :]

    def to_partner(j):
        return remote(pbuf.at[j], xbuf.at[j], p_send.at[j], p_recv.at[j], partner)

    @pl.loop(0, 4)
    def _(j):
        pbuf[j] = dot(gated_ref[...], w_block(j, 1 - core), 1, 1).astype(BF16)
        to_partner(j).start()

    @pl.loop(0, 4)
    def _(j):
        pacc[j] = dot(gated_ref[...], w_block(j, core), 1, 1)

    @pl.loop(0, 4)
    def _(j):
        to_partner(j).wait_recv()
        pacc[j] += xbuf[j].astype(F32)

    def rs_right(j, h):
        return remote(snd_r.at[j, half(h)], rec_l.at[j, half(h)], rr_send.at[j, h], rr_recv.at[j, h], right)

    def rs_left(j, h):
        return remote(snd_l.at[j, half(h)], rec_r.at[j, half(h)], rl_send.at[j, h], rl_recv.at[j, h], left)

    def rs_first(m, h):
        jr, jl = 3 - m, m

        @pl.when(zl == 0)
        def _():
            snd_r[jr, half(h)] = pacc[jr, half(h)].astype(BF16)
            rs_right(jr, h).start()

        @pl.when(zl == 3)
        def _():
            snd_l[jl, half(h)] = pacc[jl, half(h)].astype(BF16)
            rs_left(jl, h).start()

    def rs_hop(m, h):
        jr, jl = 3 - m, m

        @pl.when(jnp.logical_and(jr > zl, zl > 0))
        def _():
            rs_right(jr, h).wait_recv()
            snd_r[jr, half(h)] = (pacc[jr, half(h)] + rec_l[jr, half(h)].astype(F32)).astype(BF16)
            rs_right(jr, h).start()

        @pl.when(jnp.logical_and(jl < zl, zl < 3))
        def _():
            rs_left(jl, h).wait_recv()
            snd_l[jl, half(h)] = (pacc[jl, half(h)] + rec_r[jl, half(h)].astype(F32)).astype(BF16)
            rs_left(jl, h).start()

    for m in range(3):
        for h in range(2):
            rs_first(m, h)

    def back_own(j):
        back_ref[...] += dot(g_own[j], w_block(j, core))

    def back_par(j):
        for h in range(2):
            ag_partner(d_ref, j, h).wait_recv()
        back_ref[...] += dot(g_par[j], w_block(j, 1 - core))

    def both_sides(act, m):
        @pl.when(zl - m >= 0)
        def _():
            act(zl - m)

        @pl.when(zl + m <= 3)
        def _():
            act(zl + m)

    ag_step(2, 1)
    back_ref[...] = dot(g_own[zl], w_block(zl, core))
    back_par(zl)
    taps_tile(0)
    rs_hop(0, 0)
    both_sides(back_own, 1)
    both_sides(back_par, 1)
    ag_step(3, 0)
    rs_hop(0, 1)
    taps_tile(1)
    both_sides(back_own, 2)
    both_sides(back_par, 2)
    ag_step(3, 1)
    both_sides(back_own, 3)
    rs_hop(1, 0)
    both_sides(back_par, 3)

    dconv_ref[...] = (q_ref[...].astype(F32) * back_ref[...]).astype(BF16)
    for tile in range(2):
        part = slice(tile * 256, tile * 256 + 256)
        dt = dconv_ref[:, part]
        state_q[:, part] = fold(dot(e_q[0, part, :], dt) + dot(e_q[1, part, :], dt))
    bz = remote(state_q, zin_q, fz_send.at[2], fz_recv.at[2], zpeer)
    bz.start()
    rs_hop(1, 1)
    for tile in range(2):
        part = slice(tile * 256, tile * 256 + 256)
        state_q1[:, part] = fold(dot(e_q1[part, :], dconv_ref[:, part]))

    centre16 = (iota((16, 256), 1) - 128).astype(F32)

    def mixed_tile(tile):
        part = slice(tile * 256, tile * 256 + 256)

        @pl.loop(0, 4)
        def _(i):
            for k in range(4):
                at = tile * 16 + 4 * i + k
                mixed = jnp.where(token >= other, dot(dconv_ref[:, part], z_mask[at], 1, 1), 0.0)
                sums = dot(tab_m[at], mixed.astype(BF16), 1, 1)
                rows = pl.ds(pl.multiple_of(at * 16, 16), 16)
                fall = col_u[rows, :]
                prod_res[rows, :] = fall * sums[0:16]
                prod_rate[rows, :] = fall * (centre16 * sums[0:16] - sums[16:32])

    def dz_tile(tile):
        part = slice(tile * 256, tile * 256 + 256)

        @pl.loop(0, 8)
        def _(i):
            for g in (2 * i, 2 * i + 1):
                at = tile * 16 + g
                dz_ref[:, part] = jnp.where(
                    lane_group == g, dot(taps_back[at], dconv_ref[:, part]), dz_ref[:, part]
                )

    mixed_tile(0)
    rs_hop(2, 0)
    mixed_tile(1)
    rs_hop(2, 1)

    pick_pole = jnp.where(own_row, 1.0, 0.0).astype(F32)
    pick_group = lax.div(iota((512, 32), 0), 16) == iota((512, 32), 1)

    def param_sum(prod, cross):
        column = jnp.sum(prod[...], axis=1, keepdims=True)
        return dot_exact(pick_pole, jnp.where(pick_group, column, 0.0)) + dot_exact(cross, sel_row, 1, 1)

    gsum[0] = jnp.zeros((32, 128), F32)
    gsum[0, 0:16, 0:32] = param_sum(prod_res, state_q[...] * in_s[...])
    gsum[0, 16:32, 0:32] = param_sum(prod_rate, state_q1[...] * in_s[...] + state_q[...] * in_p[...])

    def exchange(src, dst, at, peers):
        copies = []
        for i, dev in enumerate(peers):
            copies.append(remote(src, dst.at[i], gs_send.at[at + i], gs_recv.at[at + i], dev))
            copies[-1].start()
        return copies

    started = exchange(gsum.at[0], gin_y, 0, ypeer)
    dz_tile(0)

    bz.wait_recv()
    q_one = jnp.where(first, state_q[...], zin_q[...])
    q_two = jnp.where(first, zin_q[...], state_q[...])
    pair_q[...] = q_one + slab_decay * q_two
    bx = []
    for i in range(3):
        bx.append(remote(pair_q, xin_q.at[i], bx_send.at[i], bx_recv.at[i], xpeer[i]))
        bx[-1].start()

    for c in started:
        c.wait_recv()
    gsum[1] = gsum[0] + gin_y[0] + gin_y[1] + gin_y[2]
    last = exchange(gsum.at[1], gin_c, 3, cpeer)

    dz_tile(1)
    gq_ref[...] = (conv_ref[...] * back_ref[...]).astype(BF16)

    for c in bx:
        c.wait_recv()
    sum_q = jnp.where(first, zin_q[...], 0.0)
    for i in range(3):
        steps = 4 - (i + 1)
        later = xx + steps <= 3
        gap = 256.0 * (2 * (steps - 1) + 1 - zh).astype(F32)
        sum_q += jnp.where(later, jnp.exp(-gap * rate_chan[...]) * xin_q[i], 0.0)
    in_q[...] = sum_q
    for tile in range(2):
        part = slice(tile * 256, tile * 256 + 256)
        dz = dz_ref[:, part] + carried(row_b, in_q, part)
        gv_ref[:, part] = (dz * k_ref[:, part].astype(F32)).astype(BF16)
        gk_ref[:, part] = (dz * v_ref[:, part].astype(F32)).astype(BF16)

    for c in last:
        c.wait_recv()
    total = gsum[1]
    for i in range(7):
        total += gin_c[i]
    gres_ref[...] = total[0:16, 0:32]
    grate_ref[...] = -res_ref[...] * total[16:32, 0:32]

    for h in range(2):
        @pl.when(has_left)
        def _():
            rs_right(zl, h).wait_recv()
            pacc[zl, half(h)] += rec_l[zl, half(h)].astype(F32)

        @pl.when(has_right)
        def _():
            rs_left(zl, h).wait_recv()
            pacc[zl, half(h)] += rec_r[zl, half(h)].astype(F32)

    out_ref[...] = pacc[zl].astype(BF16)

    for c in fz + fx + bx + [bz] + started + last:
        c.wait_send()
    ag_drain()
    for j in range(4):
        to_partner(j).wait_send()
        for h in range(2):
            @pl.when(j > zl)
            def _():
                rs_right(j, h).wait_send()

            @pl.when(j < zl)
            def _():
                rs_left(j, h).wait_send()


def hand_over(*refs):
    half_way = len(refs) // 2
    for src, dst in zip(refs[:half_way], refs[half_way:]):
        dst[...] = src[...]


def per_device(values_in, keys_in, query_in, cotangent, out_weight, residues, rates):
    vm = pltpu.VMEM
    dma = pltpu.SemaphoreType.DMA
    act = jax.ShapeDtypeStruct((256, 512), BF16)
    par = jax.ShapeDtypeStruct((16, 32), F32)
    spec = pl.BlockSpec(memory_space=pltpu.VMEM)
    blocks = lambda: vm((4, 256, 512), BF16)
    state = lambda: vm((16, 512), F32)
    states = lambda: vm((3, 16, 512), F32)
    scratch = [
        vm((4096, 512), BF16), dma, dma,
        vm((512, 128), F32), vm((512, 128), F32), vm((1, 512), F32), vm((1, 512), F32), state(),
        vm((32, 48, 256), BF16), vm((32, 48, 256), BF16), vm((32, 32, 256), BF16), vm((512, 256), F32),
        vm((32, 256, 256), BF16), vm((32, 256, 256), BF16), vm((512, 256), F32), vm((512, 256), F32),
        vm((2, 512, 256), BF16), vm((512, 256), BF16), vm((2, 512, 256), BF16), vm((512, 256), BF16),
        vm((2, 256, 512), BF16), vm((2, 256, 512), BF16),
        vm((256, 512), BF16), vm((256, 512), F32), vm((256, 512), BF16), vm((256, 512), BF16),
        vm((256, 512), F32), vm((256, 512), F32),
        state(), state(), state(), state(), state(), state(), states(), states(), state(), state(),
        state(), state(), state(), state(), states(), state(),
        blocks(), blocks(), vm((4, 256, 512), F32), blocks(), blocks(), blocks(), blocks(), blocks(), blocks(),
        vm((2, 32, 128), F32), vm((3, 32, 128), F32), vm((7, 32, 128), F32),
        dma((2, 3, 2)), dma((4, 2)), dma((4, 2)), dma((4, 2)),
        dma((3,)), dma((3,)), dma((2, 3)), dma((2, 3)), dma((3,)), dma((3,)),
        dma((4,)), dma((4,)), dma((4, 2)), dma((4, 2)), dma((4, 2)), dma((4, 2)), dma((10,)), dma((10,)),
    ]
    shapes = (act, act, act, act, par, par)
    results = pl.pallas_call(
        kernel,
        out_shape=shapes,
        in_specs=[spec, spec, spec, spec, pl.BlockSpec(memory_space=pl.ANY), spec, spec],
        out_specs=(spec,) * 6,
        scratch_shapes=scratch,
        compiler_params=pltpu.CompilerParams(
            collective_id=0, has_side_effects=True, vmem_limit_bytes=60 * 1024 * 1024
        ),
        name="hyena",
    )(values_in[0], keys_in[0], query_in[0], cotangent[0], out_weight, rates, residues)
    out, gv, gk, gq, gres, grate = pl.pallas_call(
        hand_over, out_shape=shapes, in_specs=[spec] * 6, out_specs=(spec,) * 6, name="results"
    )(*results)
    return out[None], gv[None], gk[None], gq[None], gres, grate


def solution(mesh):
    act = P("rep", "ctx", "chan")
    par = P(None, "chan")
    return jax.shard_map(
        per_device,
        mesh=mesh,
        in_specs=(act, act, act, act, par, par, par),
        out_specs=(act, act, act, act, par, par),
        check_vma=False,
    )
```

```python
import functools

import jax
import jax.numpy as jnp
from jax import lax
from jax.experimental import pallas as pl
from jax.experimental.pallas import tpu as pltpu
from jax.sharding import PartitionSpec as P

GROUP = 16
F32 = jnp.float32
BF16 = jnp.bfloat16
MESH = pl.DeviceIdType.MESH


def iota(shape, axis):
    return lax.broadcasted_iota(jnp.int32, shape, axis)


def dot(a, b, ca=1, cb=0):
    return lax.dot_general(a, b, (((ca,), (cb,)), ((), ())), preferred_element_type=F32)


def dot_exact(a, b, ca=1, cb=0):
    return lax.dot_general(
        a, b, (((ca,), (cb,)), ((), ())), precision=lax.Precision.HIGHEST, preferred_element_type=F32
    )


def split(a):
    high = a.astype(BF16)
    return high, (a - high.astype(F32)).astype(BF16)


def kernel(
    v_ref, k_ref, q_ref, d_ref, w_hbm, rates_ref, res_ref,
    out_ref, gv_ref, gk_ref, gq_ref, gres_ref, grate_ref,
    w_ref, w_sem, own_sem,
    rate_col, res_col, rate_row, res_row, rate_chan,
    tab_u, tab_v, tab_m, col_u, taps_back, z_mask, prod_res, prod_rate,
    e_s, e_p, e_q, e_q1, row_f, row_b,
    z_ref, conv_ref, gated_ref, dconv_ref, back_ref, dz_ref,
    state_s, state_p, pair_s, pair_p, zin_s, zin_p, xin_s, xin_p, in_s, in_p,
    state_q, state_q1, pair_q, zin_q, xin_q, in_q,
    g_own, g_par, pacc, pbuf, xbuf, snd_n, rec_n, snd_f, rec_f,
    gsum, gin_y, gin_c,
    ag_send, ag_recv, agp_send, agp_recv,
    fz_send, fz_recv, fx_send, fx_recv, bx_send, bx_recv,
    p_send, p_recv, rn_send, rn_recv, rf_send, rf_recv, gs_send, gs_recv,
):
    chan = lax.axis_index("chan")
    ctx = lax.axis_index("ctx")
    rep = lax.axis_index("rep")
    core, zl = lax.rem(chan, 2), lax.div(chan, 2)
    zh, xx = lax.rem(ctx, 2), lax.div(ctx, 2)
    near_at, far_at = zl + 1 - 2 * lax.rem(zl, 2), zl + 2 - 4 * lax.div(zl, 2)
    cross_at = near_at + 2 - 4 * lax.div(zl, 2)
    near, far = {"chan": 2 * near_at + core}, {"chan": 2 * far_at + core}
    partner = {"chan": chan + 1 - 2 * core}
    zpeer = {"ctx": ctx + 1 - 2 * zh}
    xpeer = [{"ctx": lax.rem(xx + i, 4) * 2 + zh} for i in (1, 2, 3)]
    cpeer = [{"ctx": lax.rem(ctx + i, 8)} for i in range(1, 8)]
    ypeer = [{"rep": lax.rem(rep + i, 4)} for i in (1, 2, 3)]

    def remote(src, dst, ssem, rsem, dev):
        return pltpu.make_async_remote_copy(
            src_ref=src, dst_ref=dst, send_sem=ssem, recv_sem=rsem, device_id=dev, device_id_type=MESH
        )

    w_copy = pltpu.make_async_copy(w_hbm, w_ref, w_sem)
    w_copy.start()
    own_copy = pltpu.make_async_copy(d_ref, g_own.at[zl], own_sem)
    own_copy.start()
    barrier = pltpu.get_barrier_semaphore()
    for dev in [partner, near, far] + cpeer + ypeer:
        pl.semaphore_signal(barrier, inc=1, device_id=dev, device_id_type=MESH)

    sel_row = jnp.where(lax.div(iota((32, 512), 1), 16) == iota((32, 512), 0), 1.0, 0.0).astype(F32)
    own_row = lax.rem(iota((16, 512), 1), 16) == iota((16, 512), 0)
    for src, col, row in ((rates_ref, rate_col, rate_row), (res_ref, res_col, res_row)):
        flat = dot_exact(src[...], sel_row)
        line = jnp.sum(jnp.where(own_row, flat, 0.0), axis=0, keepdims=True)
        row[...] = line
        col[...] = jnp.transpose(jnp.broadcast_to(line, (128, 512)))
        if src is rates_ref:
            rate_chan[...] = flat

    def wide(ref, rows):
        return jnp.concatenate([ref[rows, :], ref[rows, :]], axis=1)

    lane256 = iota((64, 256), 1).astype(F32)

    @pl.loop(0, 8)
    def _(i):
        rows = pl.ds(pl.multiple_of(i * 64, 64), 64)
        rate = wide(rate_col, rows)
        left_over = 256.0 - lane256
        decay = jnp.exp(-rate * left_over)
        high, low = split(decay)
        e_s[0, rows, :] = high
        e_s[1, rows, :] = low
        e_p[rows, :] = (decay * left_over).astype(BF16)

    pl.semaphore_wait(barrier, 13)

    def half(h):
        return pl.ds(h * 128, 128)

    def to_far(h):
        return remote(d_ref.at[half(h)], g_own.at[zl, half(h)], ag_send.at[0, h], ag_recv.at[zl, h], far)

    def to_near(h):
        return remote(d_ref.at[half(h)], g_own.at[zl, half(h)], ag_send.at[1, h], ag_recv.at[zl, h], near)

    def pass_on(h):
        block = g_own.at[far_at, half(h)]
        return remote(block, block, ag_send.at[2, h], ag_recv.at[far_at, h], near)

    def ag_partner(src_ref, src, h):
        return remote(
            src_ref.at[half(h)], g_par.at[src, half(h)], agp_send.at[src, h], agp_recv.at[src, h], partner
        )

    def arrived(src, h):
        block = g_own.at[src, half(h)]
        remote(block, block, ag_send.at[2, h], ag_recv.at[src, h], near).wait_recv()

    for h in range(2):
        to_far(h).start()
    for h in range(2):
        to_near(h).start()
    for h in range(2):
        ag_partner(d_ref, zl, h).start()

    def ag_far(h):
        arrived(far_at, h)
        pass_on(h).start()
        ag_partner(g_own.at[far_at], far_at, h).start()

    def ag_take(src, h):
        arrived(src, h)
        ag_partner(g_own.at[src], src, h).start()

    def ag_drain():
        for h in range(2):
            to_far(h).wait_send()
            to_near(h).wait_send()
            pass_on(h).wait_send()
            for j in range(4):
                ag_partner(d_ref, j, h).wait_send()

    z_ref[...] = (k_ref[...].astype(F32) * v_ref[...].astype(F32)).astype(BF16)
    own_block = lax.div(iota((256, 256), 0), 16) == lax.div(iota((256, 256), 1), 16)

    def fold(a):
        return jnp.sum(jnp.where(own_block, a, 0.0).reshape(16, 16, 256), axis=0)

    def spread(s):
        return jnp.where(own_block, jnp.broadcast_to(s[None], (16, 16, 256)).reshape(256, 256), 0.0)

    for tile in range(2):
        part = slice(tile * 256, tile * 256 + 256)
        zt = z_ref[:, part]
        state_s[:, part] = fold(dot(e_s[0, part, :], zt) + dot(e_s[1, part, :], zt))
        state_p[:, part] = fold(dot(e_p[part, :], zt))

    fz = [
        remote(state_s, zin_s, fz_send.at[0], fz_recv.at[0], zpeer),
        remote(state_p, zin_p, fz_send.at[1], fz_recv.at[1], zpeer),
    ]
    for c in fz:
        c.start()

    @pl.loop(0, 8)
    def _(i):
        rows = pl.ds(pl.multiple_of(i * 64, 64), 64)
        groups = pl.ds(i * 4, 4)
        rate, res = wide(rate_col, rows), wide(res_col, rows)
        centre = lane256 - 128.0
        fall, rise = jnp.exp(-rate * centre), jnp.exp(rate * centre)
        u_high, u_low = split(res * fall)
        v_high, v_low = split(rise)
        for at, uu, vv in ((0, u_high, v_high), (16, u_high, v_low), (32, u_low, v_high)):
            tab_u[groups, at : at + 16, :] = uu.reshape(4, 16, 256)
            tab_v[groups, at : at + 16, :] = vv.reshape(4, 16, 256)
        tab_m[groups, 0:16, :] = v_high.reshape(4, 16, 256)
        tab_m[groups, 16:32, :] = (rise * centre).astype(BF16).reshape(4, 16, 256)
        col_u[rows, :] = fall

    token = iota((256, 256), 0)
    other = iota((256, 256), 1)
    lane_group = lax.div(other, 16)

    def conv_tile(tile, low, high):
        part = slice(tile * 256, tile * 256 + 256)

        @pl.loop(low, high)
        def _(i):
            for g in (2 * i, 2 * i + 1):
                at = tile * 16 + g
                taps = jnp.where(token >= other, dot(tab_u[at], tab_v[at], 0, 0), 0.0).astype(BF16)
                conv_ref[:, part] = jnp.where(
                    lane_group == g, dot(taps, z_ref[:, part]), conv_ref[:, part]
                )

    def taps_tile(tile):
        part = slice(tile * 256, tile * 256 + 256)

        @pl.loop(0, 8)
        def _(i):
            for g in (2 * i, 2 * i + 1):
                at = tile * 16 + g
                taps = jnp.where(other >= token, dot(tab_v[at], tab_u[at], 0, 0), 0.0)
                taps_back[at] = taps.astype(BF16)
                z_mask[at] = jnp.where(lane_group == g, z_ref[:, part].astype(F32), 0.0).astype(BF16)

    conv_tile(0, 0, 8)

    slab_decay = jnp.exp(-256.0 * rate_chan[...])
    for c in fz:
        c.wait_recv()
    first = zh == 0
    s_one = jnp.where(first, state_s[...], zin_s[...])
    s_two = jnp.where(first, zin_s[...], state_s[...])
    p_one = jnp.where(first, state_p[...], zin_p[...])
    p_two = jnp.where(first, zin_p[...], state_p[...])
    pair_s[...] = slab_decay * s_one + s_two
    pair_p[...] = slab_decay * (p_one + 256.0 * s_one) + p_two
    fx = []
    for i in range(3):
        fx.append(remote(pair_s, xin_s.at[i], fx_send.at[0, i], fx_recv.at[0, i], xpeer[i]))
        fx[-1].start()
    for i in range(3):
        fx.append(remote(pair_p, xin_p.at[i], fx_send.at[1, i], fx_recv.at[1, i], xpeer[i]))
        fx[-1].start()

    conv_tile(1, 0, 4)
    ag_far(0)
    conv_tile(1, 4, 8)
    ag_far(1)

    @pl.loop(0, 4)
    def _(i):
        rows = pl.ds(pl.multiple_of(i * 64, 64), 64)
        at = (iota((64, 512), 0) + i * 64).astype(F32)
        rate, res = rate_row[...], res_row[...]
        f_high, f_low = split(res * jnp.exp(-rate * at))
        row_f[0, rows, :] = f_high
        row_f[1, rows, :] = f_low
        b_high, b_low = split(res * jnp.exp(-rate * (256.0 - at)))
        row_b[0, rows, :] = b_high
        row_b[1, rows, :] = b_low

    @pl.loop(0, 8)
    def _(i):
        rows = pl.ds(pl.multiple_of(i * 64, 64), 64)
        decay = jnp.exp(-wide(rate_col, rows) * lane256)
        high, low = split(decay)
        e_q[0, rows, :] = high
        e_q[1, rows, :] = low
        e_q1[rows, :] = (decay * lane256).astype(BF16)

    for c in fx:
        c.wait_recv()
    sum_s = jnp.where(first, 0.0, zin_s[...])
    sum_p = jnp.where(first, 0.0, zin_p[...])
    for i in range(3):
        gap = 256.0 * (2 * i + zh).astype(F32)
        earlier = xx >= i + 1
        weight = jnp.exp(-gap * rate_chan[...])
        sum_s += jnp.where(earlier, weight * xin_s[i], 0.0)
        sum_p += jnp.where(earlier, weight * (xin_p[i] + gap * xin_s[i]), 0.0)
    in_s[...] = sum_s
    in_p[...] = sum_p

    def carried(rows, state, part):
        s_high, s_low = split(spread(state[:, part]))
        return (
            dot(rows[0, :, part], s_high) + dot(rows[1, :, part], s_high) + dot(rows[0, :, part], s_low)
        )

    for tile in range(2):
        part = slice(tile * 256, tile * 256 + 256)
        conv = conv_ref[:, part] + carried(row_f, in_s, part)
        conv_ref[:, part] = conv
        gated_ref[:, part] = (q_ref[:, part].astype(F32) * conv).astype(BF16)

    w_copy.wait()
    own_copy.wait()

    def w_block(j, a):
        return w_ref[pl.ds(pl.multiple_of((2 * j + a) * 512, 512), 512), :]

    def to_partner(j):
        return remote(pbuf.at[j], xbuf.at[j], p_send.at[j], p_recv.at[j], partner)

    @pl.loop(0, 4)
    def _(j):
        pbuf[j] = dot(gated_ref[...], w_block(j, 1 - core), 1, 1).astype(BF16)
        to_partner(j).start()

    @pl.loop(0, 4)
    def _(j):
        pacc[j] = dot(gated_ref[...], w_block(j, core), 1, 1)

    @pl.loop(0, 4)
    def _(j):
        to_partner(j).wait_recv()
        pacc[j] += xbuf[j].astype(F32)

    def rs_near(k, h):
        return remote(
            snd_n.at[k, half(h)], rec_n.at[k, half(h)], rn_send.at[k, h], rn_recv.at[k, h], near
        )

    def rs_far(h):
        return remote(snd_f.at[half(h)], rec_f.at[half(h)], rf_send.at[h], rf_recv.at[h], far)

    for k, j in ((0, cross_at), (1, near_at)):
        snd_n[k] = pacc[j].astype(BF16)
        for h in range(2):
            rs_near(k, h).start()

    def rs_service(h):
        rs_near(0, h).wait_recv()
        snd_f[half(h)] = (pacc[far_at, half(h)] + rec_n[0, half(h)].astype(F32)).astype(BF16)
        rs_far(h).start()

    def back_own(j):
        back_ref[...] += dot(g_own[j], w_block(j, core))

    def back_par(j):
        for h in range(2):
            ag_partner(d_ref, j, h).wait_recv()
        back_ref[...] += dot(g_par[j], w_block(j, 1 - core))

    back_ref[...] = dot(g_own[zl], w_block(zl, core))
    back_par(zl)
    for h in range(2):
        ag_take(near_at, h)
    back_own(far_at)
    back_own(near_at)
    back_par(far_at)
    taps_tile(0)
    back_par(near_at)
    ag_take(cross_at, 0)
    taps_tile(1)
    ag_take(cross_at, 1)
    back_own(cross_at)
    back_par(cross_at)

    dconv_ref[...] = (q_ref[...].astype(F32) * back_ref[...]).astype(BF16)
    for tile in range(2):
        part = slice(tile * 256, tile * 256 + 256)
        dt = dconv_ref[:, part]
        state_q[:, part] = fold(dot(e_q[0, part, :], dt) + dot(e_q[1, part, :], dt))
    bz = remote(state_q, zin_q, fz_send.at[2], fz_recv.at[2], zpeer)
    bz.start()
    rs_service(0)
    rs_service(1)
    for tile in range(2):
        part = slice(tile * 256, tile * 256 + 256)
        state_q1[:, part] = fold(dot(e_q1[part, :], dconv_ref[:, part]))

    centre16 = (iota((16, 256), 1) - 128).astype(F32)

    def mixed_tile(tile):
        part = slice(tile * 256, tile * 256 + 256)

        @pl.loop(0, 4)
        def _(i):
            for k in range(4):
                at = tile * 16 + 4 * i + k
                mixed = jnp.where(token >= other, dot(dconv_ref[:, part], z_mask[at], 1, 1), 0.0)
                sums = dot(tab_m[at], mixed.astype(BF16), 1, 1)
                rows = pl.ds(pl.multiple_of(at * 16, 16), 16)
                fall = col_u[rows, :]
                prod_res[rows, :] = fall * sums[0:16]
                prod_rate[rows, :] = fall * (centre16 * sums[0:16] - sums[16:32])

    def dz_tile(tile):
        part = slice(tile * 256, tile * 256 + 256)

        @pl.loop(0, 8)
        def _(i):
            for g in (2 * i, 2 * i + 1):
                at = tile * 16 + g
                dz_ref[:, part] = jnp.where(
                    lane_group == g, dot(taps_back[at], dconv_ref[:, part]), dz_ref[:, part]
                )

    mixed_tile(0)
    mixed_tile(1)

    bz.wait_recv()
    q_one = jnp.where(first, state_q[...], zin_q[...])
    q_two = jnp.where(first, zin_q[...], state_q[...])
    pair_q[...] = q_one + slab_decay * q_two
    bx = []
    for i in range(3):
        bx.append(remote(pair_q, xin_q.at[i], bx_send.at[i], bx_recv.at[i], xpeer[i]))
        bx[-1].start()

    pick_pole = jnp.where(own_row, 1.0, 0.0).astype(F32)
    pick_group = lax.div(iota((512, 32), 0), 16) == iota((512, 32), 1)

    def param_sum(prod, cross):
        column = jnp.sum(prod[...], axis=1, keepdims=True)
        return dot_exact(pick_pole, jnp.where(pick_group, column, 0.0)) + dot_exact(cross, sel_row, 1, 1)

    gsum[0] = jnp.zeros((32, 128), F32)
    gsum[0, 0:16, 0:32] = param_sum(prod_res, state_q[...] * in_s[...])
    gsum[0, 16:32, 0:32] = param_sum(prod_rate, state_q1[...] * in_s[...] + state_q[...] * in_p[...])

    def exchange(src, dst, at, peers):
        copies = []
        for i, dev in enumerate(peers):
            copies.append(remote(src, dst.at[i], gs_send.at[at + i], gs_recv.at[at + i], dev))
            copies[-1].start()
        return copies

    started = exchange(gsum.at[0], gin_y, 0, ypeer)
    dz_tile(0)

    for c in started:
        c.wait_recv()
    gsum[1] = gsum[0] + gin_y[0] + gin_y[1] + gin_y[2]
    last = exchange(gsum.at[1], gin_c, 3, cpeer)

    dz_tile(1)
    gq_ref[...] = (conv_ref[...] * back_ref[...]).astype(BF16)

    for c in bx:
        c.wait_recv()
    sum_q = jnp.where(first, zin_q[...], 0.0)
    for i in range(3):
        steps = 4 - (i + 1)
        later = xx + steps <= 3
        gap = 256.0 * (2 * (steps - 1) + 1 - zh).astype(F32)
        sum_q += jnp.where(later, jnp.exp(-gap * rate_chan[...]) * xin_q[i], 0.0)
    in_q[...] = sum_q
    for tile in range(2):
        part = slice(tile * 256, tile * 256 + 256)
        dz = dz_ref[:, part] + carried(row_b, in_q, part)
        gv_ref[:, part] = (dz * k_ref[:, part].astype(F32)).astype(BF16)
        gk_ref[:, part] = (dz * v_ref[:, part].astype(F32)).astype(BF16)

    for h in range(2):
        rs_near(1, h).wait_recv()
        rs_far(h).wait_recv()
    out_ref[...] = (pacc[zl] + rec_n[1].astype(F32) + rec_f[...].astype(F32)).astype(BF16)

    for c in last:
        c.wait_recv()
    total = gsum[1]
    for i in range(7):
        total += gin_c[i]
    gres_ref[...] = total[0:16, 0:32]
    grate_ref[...] = -res_ref[...] * total[16:32, 0:32]

    for c in fz + fx + bx + [bz] + started + last:
        c.wait_send()
    ag_drain()
    for j in range(4):
        to_partner(j).wait_send()
    for h in range(2):
        rs_near(0, h).wait_send()
        rs_near(1, h).wait_send()
        rs_far(h).wait_send()


def hand_over(*refs):
    half_way = len(refs) // 2
    for src, dst in zip(refs[:half_way], refs[half_way:]):
        dst[...] = src[...]


def per_device(values_in, keys_in, query_in, cotangent, out_weight, residues, rates):
    vm = pltpu.VMEM
    dma = pltpu.SemaphoreType.DMA
    act = jax.ShapeDtypeStruct((256, 512), BF16)
    par = jax.ShapeDtypeStruct((16, 32), F32)
    spec = pl.BlockSpec(memory_space=pltpu.VMEM)
    blocks = lambda: vm((4, 256, 512), BF16)
    state = lambda: vm((16, 512), F32)
    states = lambda: vm((3, 16, 512), F32)
    scratch = [
        vm((4096, 512), BF16), dma, dma,
        vm((512, 128), F32), vm((512, 128), F32), vm((1, 512), F32), vm((1, 512), F32), state(),
        vm((32, 48, 256), BF16), vm((32, 48, 256), BF16), vm((32, 32, 256), BF16), vm((512, 256), F32),
        vm((32, 256, 256), BF16), vm((32, 256, 256), BF16), vm((512, 256), F32), vm((512, 256), F32),
        vm((2, 512, 256), BF16), vm((512, 256), BF16), vm((2, 512, 256), BF16), vm((512, 256), BF16),
        vm((2, 256, 512), BF16), vm((2, 256, 512), BF16),
        vm((256, 512), BF16), vm((256, 512), F32), vm((256, 512), BF16), vm((256, 512), BF16),
        vm((256, 512), F32), vm((256, 512), F32),
        state(), state(), state(), state(), state(), state(), states(), states(), state(), state(),
        state(), state(), state(), state(), states(), state(),
        blocks(), blocks(), vm((4, 256, 512), F32), blocks(), blocks(),
        vm((2, 256, 512), BF16), vm((2, 256, 512), BF16), vm((256, 512), BF16), vm((256, 512), BF16),
        vm((2, 32, 128), F32), vm((3, 32, 128), F32), vm((7, 32, 128), F32),
        dma((3, 2)), dma((4, 2)), dma((4, 2)), dma((4, 2)),
        dma((3,)), dma((3,)), dma((2, 3)), dma((2, 3)), dma((3,)), dma((3,)),
        dma((4,)), dma((4,)), dma((2, 2)), dma((2, 2)), dma((2,)), dma((2,)), dma((10,)), dma((10,)),
    ]
    shapes = (act, act, act, act, par, par)
    results = pl.pallas_call(
        kernel,
        out_shape=shapes,
        in_specs=[spec, spec, spec, spec, pl.BlockSpec(memory_space=pl.ANY), spec, spec],
        out_specs=(spec,) * 6,
        scratch_shapes=scratch,
        compiler_params=pltpu.CompilerParams(
            collective_id=0, has_side_effects=True, vmem_limit_bytes=60 * 1024 * 1024
        ),
        name="hyena",
    )(values_in[0], keys_in[0], query_in[0], cotangent[0], out_weight, rates, residues)
    out, gv, gk, gq, gres, grate = pl.pallas_call(
        hand_over, out_shape=shapes, in_specs=[spec] * 6, out_specs=(spec,) * 6, name="results"
    )(*results)
    return out[None], gv[None], gk[None], gq[None], gres, grate


def solution(mesh):
    act = P("rep", "ctx", "chan")
    par = P(None, "chan")
    return jax.shard_map(
        per_device,
        mesh=mesh,
        in_specs=(act, act, act, act, par, par, par),
        out_specs=(act, act, act, act, par, par),
        check_vma=False,
    )
```
